256 devices in a mesh: col: 64 (over y, z, core), row: 4 (over x).
Axes of the slice: x: 4, y: 4, z: 8, core: 2. Of those that a mesh axis runs over, the one named last changes fastest.
Arguments:
- tile_left: bfloat16 [64, 8, 1024, 64], P('col', 'row'), may hold values from -0.41992188 to 0.41992188
- tile_right: bfloat16 [64, 8, 1024, 64], P('col', 'row'), may hold values from -0.1875 to 0.1875
- row_left: bfloat16 [64, 1024, 64], P('col'), may hold values from -0.41992188 to 0.41992188
- row_right: bfloat16 [64, 1024, 64], P('col'), may hold values from -0.1875 to 0.1875
- sketch: bfloat16 [1024, 64], replicated, may hold values from -6 to 6
- panel_left: bfloat16 [8, 1024, 64], P('row'), may hold values from -0.375 to 0.375
- panel_right: bfloat16 [8, 1024, 64], P('row'), may hold values from -0.1875 to 0.1875
- pivot_inverse: bfloat16 [1024, 1024], replicated, as said below
- band_inverse: bfloat16 [8, 1024, 1024], P('row'), as said below
- link_left: bfloat16 [8, 1024, 64], P('row'), may hold values from -0.75 to 0.75
- link_right: bfloat16 [8, 1024, 64], P('row'), may hold values from -0.0625 to 0.0625
- pivot_rhs: bfloat16 [1024, 32768], P(None, 'col'), may hold values from -6 to 6
- band_rhs: bfloat16 [8, 1024, 32768], P('row', None, 'col'), may hold values from -6 to 6
- carry_in: float32 [64, 32768], P(None, 'col'), may hold values from -3 to 3
Outputs:
- pivot_solution: bfloat16 [1024, 32768], P(None, 'col')
- schur_right: float32 [8, 1024, 64], P('row', 'col')
- band_solution: bfloat16 [8, 1024, 32768], P('row', None, 'col')
- link_states: float32 [8, 64, 32768], P('row', None, 'col')
The draws below stay inside these ranges and needn't reach their ends.
Inputs may be any that keep to these rules, and one draw needn't show every extreme that they name: `pivot_inverse`: each tile is lower triangular with a positive diagonal, the inverse of a Cholesky factor of a diagonal covariance tile. `band_inverse`: each tile is lower triangular with a positive diagonal, the inverse of a Cholesky factor of a diagonal covariance tile.
All inputs are finite; a program needn't handle non-finite values.
Results may differ from the reference program's by a relative error of at most 0.0056.
Values sent between devices are 32-bit elements; how exact they have to be, the bound alone decides.
A program may use at most 128 MiB of HBM per device.

```python
import jax
import jax.numpy as jnp
from jax import lax

NB = 1024
R = 64
NJ = 64
NBR = 8
RHS_TOT = 32768


def triangle_tiles(key, tile_count):
    diag_key, off_key = jax.random.split(key)
    diagonal = jax.random.uniform(diag_key, (tile_count, NB), jnp.float32, 0.6, 1.5)
    off_diagonal = jnp.clip(jax.random.normal(off_key, (tile_count, NB, NB), jnp.float32), -4.0, 4.0) * (0.5 / NB ** 0.5)
    lower_part = jnp.tril(off_diagonal, -1)
    return lower_part + diagonal[:, :, None] * jnp.eye(NB, dtype=jnp.float32)


def draw_pivot_inverse(key, part):
    return triangle_tiles(jax.random.fold_in(key, 11), 1)[0].astype(jnp.bfloat16)


def draw_band_inverse(key, part):
    return triangle_tiles(jax.random.fold_in(key, 23), NBR).astype(jnp.bfloat16)


def steps_of(own_key, extent, shards, smallest, largest):
    def one(dim, blocks):
        draws = jax.random.uniform(jax.random.fold_in(jax.random.fold_in(own_key, 6), dim), (blocks,), jnp.float32, smallest / len(shards), largest / len(shards))
        return jnp.repeat(jnp.exp(draws), extent[dim] // blocks).reshape((-1,) + (1,) * (len(extent) - dim - 1))

    factor_of = one(*shards[0])
    for cut in shards[1:]:
        factor_of = factor_of * one(*cut)
    return factor_of


def normal_values(own_key, extent, deviation, most, cuts=(), kind=jnp.bfloat16):
    loudness = steps_of(own_key, extent, cuts, -0.22, 0.18) if cuts else 1.0
    values = jax.random.normal(own_key, extent, jnp.float32) * deviation * loudness
    return jnp.minimum(jnp.maximum(values, -most), most).astype(kind)


def setup_inputs(seed: int = 0) -> dict:
    keys = jax.random.split(jax.random.key(seed), 15)
    return {
        "tile_left": normal_values(keys[0], (NJ, NBR, NB, R), 0.07, 0.41992188, ((0, 64), (1, 4))),
        "tile_right": normal_values(keys[1], (NJ, NBR, NB, R), NB ** -0.5, 0.1875, ((0, 64), (1, 4))),
        "row_left": normal_values(keys[2], (NJ, NB, R), 0.07, 0.41992188, ((0, 64),)),
        "row_right": normal_values(keys[3], (NJ, NB, R), NB ** -0.5, 0.1875, ((0, 64),)),
        "sketch": normal_values(keys[4], (NB, R), 1.0, 6.0),
        "panel_left": normal_values(keys[5], (NBR, NB, R), (4 * R) ** -0.5, 0.375, ((0, 4),)),
        "panel_right": normal_values(keys[6], (NBR, NB, R), NB ** -0.5, 0.1875, ((0, 4),)),
        "pivot_inverse": draw_pivot_inverse(jax.random.fold_in(keys[14], 71), 0),
        "band_inverse": draw_band_inverse(jax.random.fold_in(keys[14], 71), 0),
        "link_left": normal_values(keys[9], (NBR, NB, R), R ** -0.5, 0.75, ((0, 4),)),
        "link_right": normal_values(keys[10], (NBR, NB, R), (8 * NB) ** -0.5, 0.0625, ((0, 4),)),
        "pivot_rhs": normal_values(keys[11], (NB, RHS_TOT), 1.0, 6.0, ((1, 64),)),
        "band_rhs": normal_values(keys[12], (NBR, NB, RHS_TOT), 1.0, 6.0, ((0, 4), (2, 64))),
        "carry_in": normal_values(keys[13], (R, RHS_TOT), 0.5, 3.0, ((1, 64),), jnp.float32),
    }


HIGHEST_PRECISION = lax.Precision.HIGHEST

def widened(array):
    return array.astype(jnp.float32)

def reference(tile_left, tile_right, row_left, row_right, sketch, panel_left, panel_right, pivot_inverse, band_inverse, link_left, link_right, pivot_rhs, band_rhs, carry_in):
    pivot_solution = jnp.dot(pivot_inverse.astype(jnp.float32), pivot_rhs.astype(jnp.float32), preferred_element_type=jnp.float32).astype(jnp.bfloat16)
    pulled = jnp.dot(widened(pivot_inverse).T, widened(pivot_solution), precision=HIGHEST_PRECISION)
    probe_core = jnp.einsum('jnr,ns->jrs', widened(row_left), widened(sketch), precision=HIGHEST_PRECISION)
    row_wide = widened(row_left)
    row_right_wide = widened(row_right)
    identity_matrix = jnp.eye(R, dtype=jnp.float32)

    def panel_row(band_index):
        left_tiles = widened(lax.dynamic_index_in_dim(tile_left, band_index, 1, keepdims=False))
        right_tiles = widened(lax.dynamic_index_in_dim(tile_right, band_index, 1, keepdims=False))
        coupling = jnp.einsum('jnr,jns->jrs', right_tiles, row_right_wide, precision=HIGHEST_PRECISION)
        sketch_core = jnp.einsum('jrs,jst->jrt', coupling, probe_core, precision=HIGHEST_PRECISION)
        sketched = jnp.einsum('jnr,jrt->nt', left_tiles, sketch_core, precision=HIGHEST_PRECISION)
        gram_matrix = jnp.dot(sketched.T, sketched, precision=HIGHEST_PRECISION)
        gram_lower = jnp.linalg.cholesky(gram_matrix)
        inverse_low = lax.linalg.triangular_solve(gram_lower, identity_matrix.astype(gram_lower.dtype), left_side=True, lower=True)
        panel_basis = jnp.dot(sketched, inverse_low.T, precision=HIGHEST_PRECISION)
        projected = jnp.einsum('jnr,ns->jrs', left_tiles, panel_basis, precision=HIGHEST_PRECISION)
        middle = jnp.einsum('jrs,jrt->jst', coupling, projected, precision=HIGHEST_PRECISION)
        schur = jnp.einsum('jns,jst->nt', row_wide, middle, precision=HIGHEST_PRECISION)
        return (panel_basis, schur)
    panel_basis, schur_right = lax.map(panel_row, jnp.arange(NBR, dtype=jnp.int32))

    def band_step(prior_state, items):
        inverse, right_side, left_link, right_link, left_panel, right_panel, basis_tile, schur_tile = items
        panel_coeffs = jnp.dot(widened(right_panel).T, pulled, precision=HIGHEST_PRECISION)
        schur_coeffs = jnp.dot(schur_tile.T, pulled, precision=HIGHEST_PRECISION)
        panel_term = jnp.dot(widened(left_panel), panel_coeffs, precision=HIGHEST_PRECISION) - jnp.dot(basis_tile, schur_coeffs, precision=HIGHEST_PRECISION)
        reduced = (widened(right_side) - panel_term).astype(jnp.bfloat16)
        local_part = jnp.dot(inverse.astype(jnp.float32), reduced.astype(jnp.float32), preferred_element_type=jnp.float32)
        feed_columns = jnp.dot(inverse.astype(jnp.float32), left_link.astype(jnp.float32), preferred_element_type=jnp.float32)
        solved = local_part - jnp.dot(feed_columns, prior_state, precision=HIGHEST_PRECISION)
        state = jnp.dot(widened(right_link).T, solved, precision=HIGHEST_PRECISION)
        return (state, (solved.astype(jnp.bfloat16), state))
    final_state, outputs = lax.scan(band_step, carry_in, (band_inverse, band_rhs, link_left, link_right, panel_left, panel_right, panel_basis, schur_right))
    band_solution, link_states = outputs
    return (pivot_solution, schur_right, band_solution, link_states)
```

```python
import jax
import jax.numpy as jnp
from jax import lax
from jax.experimental import pallas as pl
from jax.experimental.pallas import tpu as pltpu
from jax.sharding import PartitionSpec as P

F32 = jnp.float32
BF16 = jnp.bfloat16
HIGHEST = lax.Precision.HIGHEST
MESH = pl.DeviceIdType.MESH
NY, NZ, NX = 4, 8, 4
BLK = 256


def nn(a, b):
    return jnp.dot(a, b, preferred_element_type=F32)


def nt(a, b):
    return lax.dot_general(a, b, (((1,), (1,)), ((), ())), preferred_element_type=F32)


def tn(a, b):
    return lax.dot_general(a, b, (((0,), (0,)), ((), ())), preferred_element_type=F32)


def nn_full(a, b):
    return jnp.dot(a, b, precision=HIGHEST, preferred_element_type=F32)


def nt_full(a, b):
    return lax.dot_general(
        a, b, (((1,), (1,)), ((), ())), precision=HIGHEST, preferred_element_type=F32
    )


def high_low(a):
    high = a.astype(BF16)
    return high, (a - high.astype(F32)).astype(BF16)


def stacked_parts(a):
    return jnp.concatenate(high_low(a), axis=0)


def joined_rows(a):
    half = a.shape[0] // 2
    return a[:half] + a[half:]


def distance(k):
    return 4 + lax.div(k + 1, 2) * (1 - 2 * lax.rem(k, 2))


def kernel(
    tl_h, tr_h, rl_h, rr_h, sk_h, pl_h, pr_h, pi_h, bi_h, ll_h, lr_h, prhs_h, brhs_h, carry_h,
    ps_o, sr_o, bs_o, ls_o,
    tl, tr, rl, rr, sk, plt, prt, pi, bi, ll, lr, prhs, red, carry,
    ps, pulled, rl2, coup, vhl, pchl, l0, ms, a0, xx, sol, states, srout,
    terms1, core1, sum1, yin1, ysum1, zin1, full1,
    terms2, core2, sum2, yin2, ysum2, zin2, full2, zfull,
    yfull, yhl, qhl, chol, bt, es,
    xa_own, xn_own, xa, xn, xz_own, xz, cps, early,
    load_sem, out_sem,
    c_send, c_recv, y_send, y_recv, z_send, z_recv,
    gz_send, gz_recv, gy_send, gy_recv, gc_send, gc_recv,
    x_send, x_recv,
):
    me = lax.axis_index("col")
    x = lax.axis_index("row")
    c = lax.rem(me, 2)
    z = lax.rem(lax.div(me, 2), NZ)
    y = lax.div(me, 2 * NZ)

    def at_core():
        return {"col": (y * NZ + z) * 2 + (1 - c)}

    def at_y(dy):
        return {"col": (lax.rem(y + dy, NY) * NZ + z) * 2 + c}

    def at_z(d):
        return {"col": (y * NZ + lax.rem(z + d, NZ)) * 2 + c}

    def at_x(d):
        return {"row": lax.rem(x + d, NX)}

    loads = [
        pltpu.make_async_copy(src, dst, load_sem.at[i])
        for i, (src, dst) in enumerate(
            [
                (tr_h, tr), (rr_h, rr), (sk_h, sk), (rl_h, rl), (tl_h, tl),
                (pi_h, pi), (prhs_h, prhs), (lr_h, lr), (bi_h, bi), (ll_h, ll),
                (pr_h, prt), (pl_h, plt), (brhs_h, red), (carry_h, carry),
            ]
        )
    ]
    for i in range(5):
        loads[i].start()

    barrier = pltpu.get_barrier_semaphore()
    peers = [at_core()]
    peers += [at_y(d) for d in range(1, NY)]
    peers += [at_z(d) for d in range(1, NZ)]
    peers += [at_x(d) for d in range(1, NX)]
    for peer in peers:
        pl.semaphore_signal(barrier, inc=1, device_id=peer, device_id_type=MESH)

    def remote(src, dst, send, recv, device):
        return pltpu.make_async_remote_copy(
            src_ref=src, dst_ref=dst, send_sem=send, recv_sem=recv,
            device_id=device, device_id_type=MESH,
        )

    def reduce_scatter(s, terms, core, total, yin, ysum, zin):
        def core_copy(k):
            zt = lax.rem(z + distance(k), NZ)
            return remote(
                terms.at[(1 - c) * NZ + zt], core.at[zt], c_send.at[s, k], c_recv.at[s, k], at_core()
            )

        def y_copy(k, dy):
            zt = lax.rem(z + distance(k), NZ)
            return remote(
                total.at[zt, lax.rem(y + dy, NY)], yin.at[k, dy - 1],
                y_send.at[s, k, dy - 1], y_recv.at[s, k, dy - 1], at_y(dy),
            )

        def z_copy(k):
            return remote(
                ysum.at[k], zin.at[k], z_send.at[s, k], z_recv.at[s, k], at_z(distance(k))
            )

        def send_core():
            def step(k, carried):
                core_copy(k).start()
                return carried

            lax.fori_loop(0, NZ, step, 0)

        def fold_core():
            def step(k, carried):
                core_copy(k).wait_recv()
                zt = lax.rem(z + distance(k), NZ)
                total[zt] = terms[c * NZ + zt] + core[zt]
                for dy in range(1, NY):
                    y_copy(k, dy).start()
                return carried

            lax.fori_loop(0, NZ, step, 0)

        def y_total(k):
            for dy in range(1, NY):
                y_copy(k, dy).wait_recv()
            zt = lax.rem(z + distance(k), NZ)
            return (total[zt, y] + yin[k, 0]) + (yin[k, 1] + yin[k, 2])

        def fold_y():
            def step(k, carried):
                ysum[k] = y_total(k)
                z_copy(k).start()
                return carried

            lax.fori_loop(0, NZ - 1, step, 0)
            ysum[NZ - 1] = y_total(NZ - 1)

        def fold_z():
            block = ysum[NZ - 1]
            for k in range(NZ - 2, -1, -1):
                z_copy(k).wait_recv()
                block = block + zin[k]
            return block

        def finish():
            def step(k, carried):
                core_copy(k).wait_send()
                for dy in range(1, NY):
                    y_copy(k, dy).wait_send()
                return carried

            lax.fori_loop(0, NZ, step, 0)

            def step_z(k, carried):
                z_copy(k).wait_send()
                return carried

            lax.fori_loop(0, NZ - 1, step_z, 0)

        return send_core, fold_core, fold_y, fold_z, finish

    def all_gather(s, full):
        def z_copy(k):
            own = full.at[c * NZ + z, y]
            return remote(own, own, gz_send.at[s, k], gz_recv.at[s, k], at_z(distance(k)))

        def origin(k):
            return lax.rem(z - distance(k) + NZ, NZ)

        def z_arrival(k):
            block = full.at[c * NZ + origin(k), y]
            return remote(block, block, gz_send.at[s, k], gz_recv.at[s, k], at_z(distance(k)))

        def y_copy(k, dy):
            block = full.at[c * NZ + origin(k), y]
            return remote(
                block, block, gy_send.at[s, k, dy - 1], gy_recv.at[s, k, dy - 1], at_y(dy)
            )

        def y_arrival(k, dy):
            block = full.at[c * NZ + origin(k), lax.rem(y - dy + NY, NY)]
            return remote(
                block, block, gy_send.at[s, k, dy - 1], gy_recv.at[s, k, dy - 1], at_y(dy)
            )

        def core_copy(k):
            group = full.at[c * NZ + origin(k)]
            return remote(group, group, gc_send.at[s, k], gc_recv.at[s, k], at_core())

        def core_arrival(k):
            group = full.at[(1 - c) * NZ + origin(k)]
            return remote(group, group, gc_send.at[s, k], gc_recv.at[s, k], at_core())

        def send_z():
            def step(k, carried):
                z_copy(k).start()
                return carried

            lax.fori_loop(0, NZ - 1, step, 0)
            for dy in range(1, NY):
                y_copy(NZ - 1, dy).start()

        def pass_y():
            def step(i, carried):
                k = NZ - 2 - i
                z_arrival(k).wait_recv()
                for dy in range(1, NY):
                    y_copy(k, dy).start()
                return carried

            lax.fori_loop(0, NZ - 1, step, 0)

        def pass_core():
            def step(i, carried):
                k = NZ - 1 - i
                for dy in range(1, NY):
                    y_arrival(k, dy).wait_recv()
                core_copy(k).start()
                return carried

            lax.fori_loop(0, NZ, step, 0)

        def arrive():
            def step(i, carried):
                core_arrival(NZ - 1 - i).wait_recv()
                return carried

            lax.fori_loop(0, NZ, step, 0)

        def finish():
            def step(k, carried):
                for dy in range(1, NY):
                    y_copy(k, dy).wait_send()
                core_copy(k).wait_send()
                return carried

            lax.fori_loop(0, NZ, step, 0)

            def step_z(k, carried):
                z_copy(k).wait_send()
                return carried

            lax.fori_loop(0, NZ - 1, step_z, 0)

        return send_z, pass_y, pass_core, arrive, finish

    def x_copy(kind, d):
        src = (xa_own, xn_own, xz_own)[kind]
        dst = (xa, xn, xz)[kind].at[d - 1]
        return remote(src, dst, x_send.at[kind, d - 1], x_recv.at[kind, d - 1], at_x(d))

    rs1 = reduce_scatter(0, terms1, core1, sum1, yin1, ysum1, zin1)
    ag1 = all_gather(0, full1)
    rs2 = reduce_scatter(1, terms2, core2, sum2, yin2, ysum2, zin2)
    ag2 = all_gather(1, full2)
    ag3 = all_gather(2, zfull)

    def pivot_rows(m):
        top = (m + 1) * BLK
        block = nn(pi[m * BLK : top, :top], prhs[:top, :])
        ps[m * BLK : top, :] = block.astype(BF16)

    def pulled_rows(m):
        low, top = m * BLK, (m + 1) * BLK
        pulled[low:top, :] = tn(pi[low:, low:top], ps[low:, :]).astype(BF16)

    def link_inverse(b, m):
        low, top = m * BLK, (m + 1) * BLK
        block = nn(lr[b * 64 : (b + 1) * 64, low:], bi[b, low:, low:top])
        vhl[b, :, low:top] = stacked_parts(block)

    def panel_coeffs():
        coeffs = nn(prt[...], pulled[...])
        for b in range(2):
            pchl[b] = stacked_parts(coeffs[b * 64 : (b + 1) * 64])

    def reduce_rows(b, m):
        low, top = m * BLK, (m + 1) * BLK
        left = plt[b * 64 : (b + 1) * 64, low:top]
        term = tn(jnp.concatenate([left, left], axis=0), pchl[b])
        red[b, low:top, :] = (red[b, low:top, :].astype(F32) - term).astype(BF16)

    def local_rows(b, m):
        low, top = m * BLK, (m + 1) * BLK
        l0[b, low:top, :] = nn(bi[b, low:top, :top], red[b, :top, :])

    def chain_terms():
        for b in range(2):
            ms[b] = joined_rows(nt(vhl[b], ll[b * 64 : (b + 1) * 64, :]))
            a0[b] = joined_rows(nn(vhl[b], red[b]))
        through = nn_full(ms[1], ms[0])
        xn_own[...] = through
        first = jnp.where(x == 0, 1.0, 0.0).astype(F32)
        xa_own[...] = (
            a0[1] - nn_full(ms[1], a0[0]) + first * nn_full(through, carry[...])
        )
        for d in range(1, NX):
            x_copy(1, d).start()
            x_copy(0, d).start()

    def chain_start():
        for d in range(1, NX):
            x_copy(1, d).wait_recv()
            x_copy(0, d).wait_recv()
        flag = [jnp.where(x >= d, 1.0, 0.0).astype(F32) for d in range(NX)]
        two = flag[2] * xn[0]
        three = flag[3] * nn_full(xn[0], xn[1])
        cps[0, :64, :] = two
        cps[1, :64, :] = three
        cps[0, 64:, :] = jnp.zeros((64, 64), F32)
        cps[1, 64:, :] = jnp.zeros((64, 64), F32)
        early[...] = (
            (1.0 - flag[1]) * carry[...]
            + flag[1] * xa[0]
            + nn_full(two, xa[1])
            + nn_full(three, xa[2])
        )

    rows_i = lax.broadcasted_iota(jnp.int32, (128, 128), 0)
    cols_i = lax.broadcasted_iota(jnp.int32, (128, 128), 1)

    def gram():
        blocks = [yhl[b] for b in range(2)]
        for b in range(2):
            high, low = blocks[b][:64], blocks[b][64:]
            square = nt(high, high) + (nt(high, low) + nt(low, high))
            eye = jnp.where(
                lax.broadcasted_iota(jnp.int32, (64, 64), 0)
                == lax.broadcasted_iota(jnp.int32, (64, 64), 1),
                1.0,
                0.0,
            ).astype(F32)
            pair = [square, eye] if b == 0 else [eye, square]
            chol[b * 64 : (b + 1) * 64, :] = jnp.concatenate(pair, axis=1)

    def eliminate(first, last):
        work = [chol[b * 64 : (b + 1) * 64, :] for b in range(2)]
        done = [[], []]
        start = (first // 8) * 8
        for b in range(2):
            done[b] = work[b][:start]
            work[b] = work[b][start:]
        height = 64 - start
        row_id = lax.broadcasted_iota(jnp.int32, (height, 1), 0) + start
        for k in range(first, last):
            for b in range(2):
                lane = k + 64 * b
                body = work[b]
                pivot_row = body[k - start : k - start + 1, :]
                pivot = pivot_row[:, lane : lane + 1]
                column = body[:, lane : lane + 1]
                factor = jnp.where(row_id > k, column / pivot, 0.0)
                work[b] = body - factor * pivot_row
        for b in range(2):
            chol[b * 64 + start : (b + 1) * 64, :] = work[b]

    def factors():
        full = chol[...]
        pivots = jnp.sum(jnp.where(rows_i == cols_i, full, 0.0), axis=1, keepdims=True)
        scaled = full * lax.rsqrt(pivots)
        moved = pltpu.roll(scaled, 64, 1)
        same = (rows_i < 64) == (cols_i < 64)
        inverse = jnp.where(same, moved, 0.0)
        bt[:128, :] = inverse
        yt = jnp.concatenate([yfull[0], yfull[1]], axis=0)
        basis = nn_full(inverse, yt)
        for b in range(2):
            qhl[b] = stacked_parts(basis[b * 64 : (b + 1) * 64])
        pieces = []
        for b in range(2):
            cross = joined_rows(nt(vhl[b], qhl[b]))
            cross = cross + pltpu.roll(cross, 64, 1)
            es[b] = cross[:, :64]
        pieces = [-nn_full(ms[1], es[0]), es[1]]
        outward = nn_full(jnp.concatenate(pieces, axis=1), inverse)
        bt[128:192, :] = outward
        bt[192:, :] = jnp.zeros((64, 128), F32)

    def response_rows(b, m):
        low, top = m * BLK, (m + 1) * BLK
        right = jnp.concatenate(
            [qhl[b, :64, :top], ll[b * 64 : (b + 1) * 64, :top]], axis=0
        )
        xx[b, low:top, :] = nt(bi[b, low:top, :top], right).astype(BF16)

    for i in range(4):
        loads[i].wait()
    for i in range(5, 14):
        loads[i].start()
    coupling_t = nt(rr[...], tr[...])
    probe_t = nt(sk[...], rl[...])
    coup[...] = nt(tr[...], rr[...])
    core_t = nn_full(probe_t, coupling_t)
    loads[4].wait()
    for b in range(2):
        own = tl[b * 64 : (b + 1) * 64, :]
        parts = jnp.concatenate(high_low(core_t[:, b * 64 : (b + 1) * 64]), axis=1)
        block = nn(parts, jnp.concatenate([own, own], axis=0))
        for t in range(8):
            terms1[2 * t + b] = block[:, t * 128 : (t + 1) * 128].reshape(4, 16, 128)
    pl.semaphore_wait(barrier, len(peers))
    rs1[0]()
    wide = rl[...].astype(F32)
    rl2[...] = jnp.concatenate([wide, wide], axis=0).T.astype(BF16)
    rs1[1]()
    loads[5].wait()
    loads[6].wait()
    for m in range(4):
        pivot_rows(m)
    ps_out = pltpu.make_async_copy(ps, ps_o, out_sem.at[0])
    ps_out.start()
    rs1[2]()
    for m in range(4):
        pulled_rows(m)
    loads[10].wait()
    panel_coeffs()
    full1[c * NZ + z, y] = rs1[3]()
    ag1[0]()
    loads[7].wait()
    loads[8].wait()
    for b in range(2):
        for m in range(4):
            link_inverse(b, m)
    loads[11].wait()
    loads[12].wait()
    for b in range(2):
        for m in range(4):
            reduce_rows(b, m)
    ag1[1]()
    loads[9].wait()
    loads[13].wait()
    chain_terms()
    local_rows(0, 0)
    local_rows(0, 1)
    ag1[2]()
    local_rows(0, 2)
    ag1[3]()

    for b in range(2):
        yt = jnp.concatenate([full1[2 * t + b].reshape(64, 128) for t in range(8)], axis=1)
        yfull[b] = yt
        yhl[b] = stacked_parts(yt)
    middles = []
    for b in range(2):
        projected_t = joined_rows(nt(yhl[b], tl[b * 64 : (b + 1) * 64, :]))
        middles.append(nn_full(projected_t, coup[b * 64 : (b + 1) * 64, :]))
    middle_t = jnp.concatenate(middles, axis=0)
    terms2[...] = nt(rl2[...], jnp.concatenate(high_low(middle_t), axis=1)).reshape(16, 4, 16, 128)
    rs2[0]()
    gram()
    rs2[1]()
    for first in range(0, 32, 8):
        eliminate(first, first + 8)
    rs2[2]()
    for first in range(32, 64, 8):
        eliminate(first, first + 8)
    factors()
    chain_start()
    shard = nt_full(rs2[3](), bt[...])
    full2[c * NZ + z, y] = shard[:, :128]
    xz_own[...] = shard[:, 128:]
    for d in range(1, NX):
        x_copy(2, d).start()
    ag2[0]()
    local_rows(0, 3)
    for d in range(1, NX):
        x_copy(2, d).wait_recv()
    near = jnp.where(x >= 1, 1.0, 0.0).astype(F32)
    zfull[c * NZ + z, y] = (
        near * xz[0] + nt_full(xz[1][:, :64], cps[0]) + nt_full(xz[2][:, :64], cps[1])
    )
    ag3[0]()
    ag2[1]()
    local_rows(1, 0)
    local_rows(1, 1)
    ag3[1]()
    local_rows(1, 2)
    local_rows(1, 3)
    ag2[2]()
    for m in range(4):
        response_rows(0, m)
    ag3[2]()
    for m in range(4):
        response_rows(1, m)
    ag2[3]()
    ag3[3]()

    gathered = full2[...].reshape(1024, 128).astype(BF16)
    onward = zfull[...].reshape(1024, 128).astype(BF16)
    coeffs = tn(gathered, pulled[...])
    shift = tn(onward, pulled[...])
    mine = full2[lax.div(me, 4), lax.rem(me, 4)]
    srout[0] = mine[:, :64]
    srout[1] = mine[:, 64:]
    sr_out = pltpu.make_async_copy(srout, sr_o, out_sem.at[1])
    sr_out.start()
    prior = early[...] + shift[:64]
    bs_out = []
    for b in range(2):
        own = coeffs[b * 64 : (b + 1) * 64]
        state = a0[b] + nn_full(es[b], own) - nn_full(ms[b], prior)
        states[b] = state
        right = jnp.concatenate([own, -prior], axis=0).astype(BF16)
        for m in range(4):
            low, top = m * BLK, (m + 1) * BLK
            sol[b, low:top, :] = (l0[b, low:top, :] + nn(xx[b, low:top, :], right)).astype(BF16)
            copy = pltpu.make_async_copy(
                sol.at[b, pl.ds(low, BLK)], bs_o.at[b, pl.ds(low, BLK)], out_sem.at[3 + 4 * b + m]
            )
            copy.start()
            bs_out.append(copy)
        prior = state
    ls_out = pltpu.make_async_copy(states, ls_o, out_sem.at[2])
    ls_out.start()

    for phase in (rs1, ag1, rs2, ag2, ag3):
        phase[4]()
    for kind in range(3):
        for d in range(1, NX):
            x_copy(kind, d).wait_send()
    ps_out.wait()
    sr_out.wait()
    ls_out.wait()
    for copy in bs_out:
        copy.wait()


def flipped(array):
    return jnp.swapaxes(array, -1, -2)


def shards(
    tile_left, tile_right, row_left, row_right, sketch, panel_left, panel_right,
    pivot_inverse, band_inverse, link_left, link_right, pivot_rhs, band_rhs, carry_in,
):
    args = (
        flipped(tile_left).reshape(128, 1024),
        flipped(tile_right).reshape(128, 1024),
        flipped(row_left).reshape(64, 1024),
        flipped(row_right).reshape(64, 1024),
        flipped(sketch),
        flipped(panel_left).reshape(128, 1024),
        flipped(panel_right).reshape(128, 1024),
        pivot_inverse,
        band_inverse,
        flipped(link_left).reshape(128, 1024),
        flipped(link_right).reshape(128, 1024),
        pivot_rhs,
        band_rhs,
        carry_in,
    )
    vm = pltpu.VMEM
    comm = (16, 4, 16, 128)

    def comm_scratch():
        return [
            vm(comm, F32), vm((8, 4, 16, 128), F32), vm((8, 4, 16, 128), F32),
            vm((8, 3, 16, 128), F32), vm((8, 16, 128), F32), vm((7, 16, 128), F32), vm(comm, F32),
        ]

    scratch = [
        vm((128, 1024), BF16), vm((128, 1024), BF16), vm((64, 1024), BF16), vm((64, 1024), BF16),
        vm((64, 1024), BF16), vm((128, 1024), BF16), vm((128, 1024), BF16), vm((1024, 1024), BF16),
        vm((2, 1024, 1024), BF16), vm((128, 1024), BF16), vm((128, 1024), BF16),
        vm((1024, 512), BF16), vm((2, 1024, 512), BF16), vm((64, 512), F32),
        vm((1024, 512), BF16), vm((1024, 512), BF16), vm((1024, 128), BF16), vm((128, 64), F32),
        vm((2, 128, 1024), BF16), vm((2, 128, 512), BF16), vm((2, 1024, 512), F32),
        vm((2, 64, 64), F32), vm((2, 64, 512), F32), vm((2, 1024, 128), BF16),
        vm((2, 1024, 512), BF16), vm((2, 64, 512), F32), vm((2, 16, 64), F32),
        *comm_scratch(),
        *comm_scratch(), vm(comm, F32),
        vm((2, 64, 1024), F32), vm((2, 128, 1024), BF16), vm((2, 128, 1024), BF16),
        vm((128, 128), F32), vm((256, 128), F32), vm((2, 64, 64), F32),
        vm((64, 512), F32), vm((64, 64), F32), vm((3, 64, 512), F32), vm((3, 64, 64), F32),
        vm((16, 128), F32), vm((3, 16, 128), F32), vm((2, 128, 64), F32), vm((64, 512), F32),
    ]
    dma = pltpu.SemaphoreType.DMA
    sems = [
        dma((14,)), dma((11,)),
        dma((2, 8)), dma((2, 8)), dma((2, 8, 3)), dma((2, 8, 3)), dma((2, 7)), dma((2, 7)),
        dma((3, 7)), dma((3, 7)), dma((3, 8, 3)), dma((3, 8, 3)), dma((3, 8)), dma((3, 8)),
        dma((3, 3)), dma((3, 3)),
    ]
    anywhere = pl.BlockSpec(memory_space=pl.ANY)
    return pl.pallas_call(
        kernel,
        out_shape=(
            jax.ShapeDtypeStruct((1024, 512), BF16),
            jax.ShapeDtypeStruct((2, 16, 64), F32),
            jax.ShapeDtypeStruct((2, 1024, 512), BF16),
            jax.ShapeDtypeStruct((2, 64, 512), F32),
        ),
        in_specs=[anywhere] * 14,
        out_specs=(anywhere,) * 4,
        scratch_shapes=scratch + sems,
        compiler_params=pltpu.CompilerParams(
            collective_id=0, has_side_effects=True, vmem_limit_bytes=60 * 1024 * 1024
        ),
        name="panel_update",
    )(*args)


def solution(mesh):
    return jax.shard_map(
        shards,
        mesh=mesh,
        in_specs=(
            P("col", "row", None, None),
            P("col", "row", None, None),
            P("col", None, None),
            P("col", None, None),
            P(),
            P("row", None, None),
            P("row", None, None),
            P(),
            P("row", None, None),
            P("row", None, None),
            P("row", None, None),
            P(None, "col"),
            P("row", None, "col"),
            P(None, "col"),
        ),
        out_specs=(
            P(None, "col"),
            P("row", "col", None),
            P("row", None, "col"),
            P("row", None, "col"),
        ),
        check_vma=False,
    )
```

```python
import jax
import jax.numpy as jnp
from jax import lax
from jax.experimental import pallas as pl
from jax.experimental.pallas import tpu as pltpu
from jax.sharding import PartitionSpec as P

F32 = jnp.float32
BF16 = jnp.bfloat16
HIGHEST = lax.Precision.HIGHEST
MESH = pl.DeviceIdType.MESH
NY, NZ, NX = 4, 8, 4
BLK = 256
KERNEL_VMEM = 48 * 1024 * 1024
CLOSING_VMEM = 8 * 1024 * 1024


def nn(a, b):
    return jnp.dot(a, b, preferred_element_type=F32)


def nt(a, b):
    return lax.dot_general(a, b, (((1,), (1,)), ((), ())), preferred_element_type=F32)


def tn(a, b):
    return lax.dot_general(a, b, (((0,), (0,)), ((), ())), preferred_element_type=F32)


def nn_full(a, b):
    return jnp.dot(a, b, precision=HIGHEST, preferred_element_type=F32)


def nt_full(a, b):
    return lax.dot_general(
        a, b, (((1,), (1,)), ((), ())), precision=HIGHEST, preferred_element_type=F32
    )


def high_low(a):
    high = a.astype(BF16)
    return high, (a - high.astype(F32)).astype(BF16)


def stacked_parts(a):
    return jnp.concatenate(high_low(a), axis=0)


def joined_rows(a):
    half = a.shape[0] // 2
    return a[:half] + a[half:]


def distance(k):
    return 4 + lax.div(k + 1, 2) * (1 - 2 * lax.rem(k, 2))


def kernel(
    tl_h, tr_h, rl_h, rr_h, sk_h, pl_h, pr_h, pi_h, bi_h, ll_h, lr_h, prhs_h, brhs_h, carry_h,
    ps, srout, l0, xx, right, states,
    tl, tr, rl, rr, sk, plt, prt, pi, bi, ll, lr, prhs, red, carry,
    redlow, pulled, pulledlow, rl2, coup, vhl, pchl, ms, a0,
    terms1, core1, sum1, yin1, ysum1, zin1, full1,
    terms2, core2, sum2, yin2, ysum2, zin2, full2, zfull,
    yfull, yhl, qh, chol, bt, ey, es,
    xa_own, xn_own, xa, xn, xz_own, xz, cps, early,
    load_sem, c_recv, y_recv, z_recv, rs_send,
    gz_recv, gy_recv, gc_recv, ag_send, x_send, x_recv,
):
    me = lax.axis_index("col")
    x = lax.axis_index("row")
    c = lax.rem(me, 2)
    z = lax.rem(lax.div(me, 2), NZ)
    y = lax.div(me, 2 * NZ)

    def at_core():
        return {"col": (y * NZ + z) * 2 + (1 - c)}

    def at_y(dy):
        return {"col": (lax.rem(y + dy, NY) * NZ + z) * 2 + c}

    def at_z(d):
        return {"col": (y * NZ + lax.rem(z + d, NZ)) * 2 + c}

    def at_x(d):
        return {"row": lax.rem(x + d, NX)}

    loads = [
        pltpu.make_async_copy(src, dst, load_sem.at[i])
        for i, (src, dst) in enumerate(
            [
                (sk_h, sk), (rl_h, rl), (rr_h, rr), (tr_h, tr), (tl_h, tl),
                (pi_h, pi), (prhs_h, prhs), (lr_h, lr), (bi_h, bi), (ll_h, ll),
                (pr_h, prt), (pl_h, plt), (brhs_h, red), (carry_h, carry),
            ]
        )
    ]
    for i in range(5):
        loads[i].start()

    barrier = pltpu.get_barrier_semaphore()
    peers = [at_core()]
    peers += [at_y(d) for d in range(1, NY)]
    peers += [at_z(d) for d in range(1, NZ)]
    peers += [at_x(d) for d in range(1, NX)]
    for peer in peers:
        pl.semaphore_signal(barrier, inc=1, device_id=peer, device_id_type=MESH)

    def remote(src, dst, send, recv, device):
        return pltpu.make_async_remote_copy(
            src_ref=src, dst_ref=dst, send_sem=send, recv_sem=recv,
            device_id=device, device_id_type=MESH,
        )

    def loop(first, last, body):
        def step(k, carried):
            body(k)
            return carried

        lax.fori_loop(first, last, step, 0)

    def reduce_scatter(s, terms, core, total, yin, ysum, zin):
        send = rs_send.at[s]

        def group(k):
            return lax.rem(z + distance(k), NZ) * NY

        def core_copy(k):
            at = group(k)
            return remote(
                terms.at[pl.ds((1 - c) * 32 + at, NY)], core.at[pl.ds(at, NY)],
                send, c_recv.at[s, k], at_core(),
            )

        def y_copy(k, dy):
            return remote(
                total.at[group(k) + lax.rem(y + dy, NY)], yin.at[k, dy - 1],
                send, y_recv.at[s, k], at_y(dy),
            )

        def z_copy(k):
            return remote(ysum.at[k], zin.at[k], send, z_recv.at[s], at_z(distance(k)))

        def send_core():
            loop(0, NZ, lambda k: core_copy(k).start())

        def fold_core(first, last):
            def body(k):
                core_copy(k).wait_recv()
                at = group(k)
                total[pl.ds(at, NY)] = terms[pl.ds(c * 32 + at, NY)] + core[pl.ds(at, NY)]
                for dy in (2, 1, 3):
                    y_copy(k, dy).start()

            loop(first, last, body)

        def y_total(k):
            remote(
                yin.at[k], yin.at[k], send, y_recv.at[s, k], at_y(1)
            ).wait_recv()
            ysum[k] = (total[group(k) + y] + yin[k, 0]) + (yin[k, 1] + yin[k, 2])

        def fold_y():
            def body(k):
                y_total(k)
                z_copy(k).start()

            loop(0, NZ - 1, body)
            y_total(NZ - 1)

        def fold_z():
            remote(zin, zin, send, z_recv.at[s], at_z(1)).wait_recv()
            block = ysum[NZ - 1]
            for k in range(NZ - 1):
                block = block + zin[k]
            return block

        def finish():
            sent = terms.at[pl.ds(0, 63)]
            remote(sent, sent, send, z_recv.at[s], at_z(1)).wait_send()

        return send_core, fold_core, fold_y, fold_z, finish

    def all_gather(s, full):
        send = ag_send.at[s]

        def spot(k, side):
            return (c * NZ + lax.rem(z - distance(k) + NZ, NZ)) * NY + lax.rem(y + side, NY)

        def block_copy(at, recv, device):
            block = full.at[at]
            return remote(block, block, send, recv, device)

        def z_copy(k):
            return block_copy((c * NZ + z) * NY + y, gz_recv.at[s, k], at_z(distance(k)))

        def z_wait(k):
            block_copy(spot(k, 0), gz_recv.at[s, k], at_z(distance(k))).wait_recv()

        def spread_y(k):
            for dy in (2, 1, 3):
                block_copy(spot(k, 0), gy_recv.at[s, k], at_y(dy)).start()

        def groups(side, first, count):
            return full.at[pl.ds(((side * NZ) + first) * NY, count * NY)]

        def core_copy(k):
            group = groups(c, lax.rem(z - distance(k) + NZ, NZ), 1)
            return remote(group, group, send, gc_recv.at[s], at_core())

        def send_z():
            loop(0, NZ - 1, lambda k: z_copy(k).start())
            spread_y(NZ - 1)

        def down(first, last, body):
            loop(0, first - last + 1, lambda i: body(first - i))

        def pass_y(first, last):
            def body(k):
                z_wait(k)
                spread_y(k)

            down(first, last, body)

        def pass_core():
            def body(k):
                three = full.at[pl.ds(0, 3)]
                remote(three, three, send, gy_recv.at[s, k], at_y(1)).wait_recv()
                core_copy(k).start()

            down(NZ - 1, 0, body)

        def arrive():
            half = groups(1 - c, 0, NZ)
            remote(half, half, send, gc_recv.at[s], at_core()).wait_recv()

        def finish():
            sent = full.at[pl.ds(0, 63)]
            remote(sent, sent, send, gc_recv.at[s], at_core()).wait_send()

        return send_z, pass_y, pass_core, arrive, finish

    def x_copy(kind, d):
        src = (xa_own, xn_own, xz_own)[kind]
        dst = (xa, xn, xz)[kind].at[d - 1]
        return remote(src, dst, x_send.at[kind], x_recv.at[kind], at_x(d))

    def x_all(kind):
        dst = (xa, xn, xz)[kind]
        return remote(dst, dst, x_send.at[kind], x_recv.at[kind], at_x(1))

    rs1 = reduce_scatter(0, terms1, core1, sum1, yin1, ysum1, zin1)
    ag1 = all_gather(0, full1)
    rs2 = reduce_scatter(1, terms2, core2, sum2, yin2, ysum2, zin2)
    ag2 = all_gather(1, full2)
    ag3 = all_gather(2, zfull)
    home = (c * NZ + z) * NY + y

    def pivot_rows(m):
        top = (m + 1) * BLK
        block = nn(pi[m * BLK : top, :top], prhs[:top, :])
        ps[m * BLK : top, :] = block.astype(BF16)

    def pulled_rows(m):
        low, top = m * BLK, (m + 1) * BLK
        high, rest = high_low(tn(pi[low:, low:top], ps[low:, :]))
        pulled[low:top, :] = high
        pulledlow[low:top, :] = rest

    def link_inverse(b, m):
        low, top = m * BLK, (m + 1) * BLK
        block = nn(lr[b * 64 : (b + 1) * 64, low:], bi[b, low:, low:top])
        vhl[b, :, low:top] = stacked_parts(block)

    def panel_coeffs():
        coeffs = nn(prt[...], pulled[...]) + nn(prt[...], pulledlow[...])
        for b in range(2):
            pchl[b] = stacked_parts(coeffs[b * 64 : (b + 1) * 64])

    def reduce_rows(b, m):
        low, top = m * BLK, (m + 1) * BLK
        left = plt[b * 64 : (b + 1) * 64, low:top]
        term = tn(jnp.concatenate([left, left], axis=0), pchl[b])
        high, rest = high_low(red[b, low:top, :].astype(F32) - term)
        red[b, low:top, :] = high
        redlow[b, low:top, :] = rest

    def local_rows(b, m):
        low, top = m * BLK, (m + 1) * BLK
        own = bi[b, low:top, :top]
        l0[b, low:top, :] = nn(own, red[b, :top, :]) + nn(own, redlow[b, :top, :])

    def chain_terms():
        for b in range(2):
            ms[b] = joined_rows(nt(vhl[b], ll[b * 64 : (b + 1) * 64, :]))
            a0[b] = joined_rows(nn(vhl[b], red[b]) + nn(vhl[b], redlow[b]))
        through = nn_full(ms[1], ms[0])
        xn_own[...] = through
        first = jnp.where(x == 0, 1.0, 0.0).astype(F32)
        xa_own[...] = (
            a0[1] - nn_full(ms[1], a0[0]) + first * nn_full(through, carry[...])
        )
        for d in range(1, NX):
            x_copy(1, d).start()
            x_copy(0, d).start()

    def chain_start():
        x_all(1).wait_recv()
        x_all(0).wait_recv()
        flag = [jnp.where(x >= d, 1.0, 0.0).astype(F32) for d in range(NX)]
        two = flag[2] * xn[0]
        three = flag[3] * nn_full(xn[0], xn[1])
        cps[0, :64, :] = two
        cps[1, :64, :] = three
        cps[0, 64:, :] = jnp.zeros((64, 64), F32)
        cps[1, 64:, :] = jnp.zeros((64, 64), F32)
        early[...] = (
            (1.0 - flag[1]) * carry[...]
            + flag[1] * xa[0]
            + nn_full(two, xa[1])
            + nn_full(three, xa[2])
        )

    rows_i = lax.broadcasted_iota(jnp.int32, (128, 128), 0)
    cols_i = lax.broadcasted_iota(jnp.int32, (128, 128), 1)

    def gram():
        crosses = []
        for b in range(2):
            high, low = yhl[b, :64, :], yhl[b, 64:, :]
            square = nt(high, high) + (nt(high, low) + nt(low, high))
            eye = jnp.where(
                lax.broadcasted_iota(jnp.int32, (64, 64), 0)
                == lax.broadcasted_iota(jnp.int32, (64, 64), 1),
                1.0,
                0.0,
            ).astype(F32)
            pair = [square, eye] if b == 0 else [eye, square]
            chol[b * 64 : (b + 1) * 64, :] = jnp.concatenate(pair, axis=1)
            cross = joined_rows(nt(vhl[b], yhl[b]))
            crosses.append(cross[:, :64] + cross[:, 64:])
        ey[...] = jnp.concatenate(crosses, axis=1)

    def eliminate(first, last):
        work = [chol[b * 64 : (b + 1) * 64, :] for b in range(2)]
        start = (first // 8) * 8
        for b in range(2):
            work[b] = work[b][start:]
        height = 64 - start
        row_id = lax.broadcasted_iota(jnp.int32, (height, 128), 0) + start
        for k in range(first, last, 4):
            at = k - start
            for b in range(2):
                body = work[b]
                lane = k + 64 * b
                columns = [
                    jnp.broadcast_to(body[:, lane + j : lane + j + 1], (height, 128))
                    for j in range(4)
                ]
                rows = [body[at + j : at + j + 1, :] for j in range(4)]
                for j in range(4):
                    inverse = 1.0 / columns[j][at + j : at + j + 1, :]
                    pivot_row = rows[j] * inverse
                    below = jnp.where(row_id > k + j, columns[j], 0.0)
                    for i in range(j + 1, 4):
                        scale = columns[i][at + j : at + j + 1, :] * inverse
                        columns[i] = columns[i] - below * scale
                        rows[i] = rows[i] - columns[j][at + i : at + i + 1, :] * pivot_row
                    body = body - below * pivot_row
                work[b] = body
        for b in range(2):
            chol[b * 64 + start : (b + 1) * 64, :] = work[b]

    def factors():
        full = chol[...]
        pivots = jnp.sum(jnp.where(rows_i == cols_i, full, 0.0), axis=1, keepdims=True)
        scaled = full * lax.rsqrt(pivots)
        moved = pltpu.roll(scaled, 64, 1)
        same = (rows_i < 64) == (cols_i < 64)
        inverse = jnp.where(same, moved, 0.0)
        bt[:128, :] = inverse
        effect = nt_full(ey[...], inverse)
        es[...] = effect
        outward = jnp.concatenate([-nn_full(ms[1], effect[:, :64]), effect[:, 64:]], axis=1)
        bt[128:192, :] = nn_full(outward, inverse)
        bt[192:, :] = jnp.zeros((64, 128), F32)

    def panel_basis():
        yt = jnp.concatenate([yfull[0], yfull[1]], axis=0)
        qh[...] = nn_full(bt[:128, :], yt).astype(BF16)

    def response_rows(b, m):
        low, top = m * BLK, (m + 1) * BLK
        both = jnp.concatenate(
            [qh[b * 64 : (b + 1) * 64, :top], ll[b * 64 : (b + 1) * 64, :top]], axis=0
        )
        block = nt(bi[b, low:top, :top], both).astype(BF16)
        xx[b, low:top, :128] = block
        xx[b, low:top, 128:] = block

    for i in range(4):
        loads[i].wait()
    for i in range(5, 14):
        loads[i].start()
    probe_t = nt(sk[...], rl[...])
    core_t = nn_full(probe_t, nt(rr[...], tr[...]))
    loads[4].wait()
    for b in range(2):
        own = tl[b * 64 : (b + 1) * 64, :]
        parts = jnp.concatenate(high_low(core_t[:, b * 64 : (b + 1) * 64]), axis=1)
        block = nn(parts, jnp.concatenate([own, own], axis=0))
        for t in range(8):
            at = (2 * t + b) * 4
            terms1[at : at + 4] = block[:, t * 128 : (t + 1) * 128].reshape(4, 16, 128)
    pl.semaphore_wait(barrier, len(peers))
    rs1[0]()
    rs1[1](0, 4)
    wide = rl[...].astype(F32)
    rl2[...] = jnp.concatenate([wide, wide], axis=0).T.astype(BF16)
    coup[...] = nt(tr[...], rr[...])
    loads[5].wait()
    loads[6].wait()
    pivot_rows(0)
    rs1[1](4, NZ)
    for m in range(1, 4):
        pivot_rows(m)
    rs1[2]()
    for m in range(4):
        pulled_rows(m)
    loads[10].wait()
    panel_coeffs()
    loads[7].wait()
    loads[8].wait()
    for b in range(2):
        for m in range(4):
            link_inverse(b, m)
    loads[11].wait()
    loads[12].wait()
    full1[home] = rs1[3]()
    ag1[0]()
    for b in range(2):
        for m in range(4):
            reduce_rows(b, m)
    loads[9].wait()
    loads[13].wait()
    ag1[1](6, 3)
    chain_terms()
    ag1[1](2, 0)
    for m in range(3):
        local_rows(0, m)
    ag1[2]()
    ag1[3]()

    for b in range(2):
        yt = jnp.concatenate(
            [full1[(2 * t + b) * 4 : (2 * t + b) * 4 + 4].reshape(64, 128) for t in range(8)], axis=1
        )
        yfull[b] = yt
        yhl[b] = stacked_parts(yt)
    middles = []
    for b in range(2):
        projected_t = joined_rows(nt(yhl[b], tl[b * 64 : (b + 1) * 64, :]))
        middles.append(nn_full(projected_t, coup[b * 64 : (b + 1) * 64, :]))
    middle_t = jnp.concatenate(middles, axis=0)
    terms2[...] = nt(rl2[...], jnp.concatenate(high_low(middle_t), axis=1)).reshape(64, 16, 128)
    rs2[0]()
    rs2[1](0, 4)
    gram()
    rs2[1](4, NZ)
    for first in range(0, 32, 8):
        eliminate(first, first + 8)
    rs2[2]()
    for first in range(32, 64, 8):
        eliminate(first, first + 8)
    factors()
    shard = nt_full(rs2[3](), bt[...])
    xz_own[...] = shard[:, 128:]
    for d in range(1, NX):
        x_copy(2, d).start()
    full2[home] = shard[:, :128]
    ag2[0]()
    chain_start()
    panel_basis()
    ag2[1](6, 3)
    x_all(2).wait_recv()
    near_flag = jnp.where(x >= 1, 1.0, 0.0).astype(F32)
    onward = (
        near_flag * xz[0] + nt_full(xz[1][:, :64], cps[0]) + nt_full(xz[2][:, :64], cps[1])
    )
    zfull[home] = jnp.concatenate([onward[:8, :64], onward[8:, :64]], axis=1)
    ag3[0]()
    ag2[1](2, 0)
    local_rows(0, 3)
    local_rows(1, 0)
    ag3[1](6, 0)
    for m in range(1, 4):
        local_rows(1, m)
    ag2[2]()
    for b in range(2):
        for m in range(4):
            response_rows(b, m)
    ag2[3]()
    mine = full2[me]
    srout[0] = mine[:, :64]
    srout[1] = mine[:, 64:]
    high, rest = high_low(full2[...].reshape(1024, 128))
    coeffs = tn(high, pulled[...]) + (tn(rest, pulled[...]) + tn(high, pulledlow[...]))
    for b in range(2):
        own = coeffs[b * 64 : (b + 1) * 64]
        high, rest = high_low(own)
        right[b, :64, :] = high
        right[b, 128:192, :] = rest
        states[b] = a0[b] + nn_full(es[:, b * 64 : (b + 1) * 64], own)
    ag3[2]()
    ag3[3]()

    packed = zfull[...]
    onward = jnp.concatenate([packed[:, :, :64], packed[:, :, 64:]], axis=1).reshape(1024, 64)
    shift = joined_rows(tn(jnp.concatenate(high_low(onward), axis=1), pulled[...]))
    prior = early[...] + shift
    for b in range(2):
        high, rest = high_low(-prior)
        right[b, 64:128, :] = high
        right[b, 192:, :] = rest
        prior = states[b] - nn_full(ms[b], prior)
        states[b] = prior

    for phase in (rs1, rs2, ag1, ag2, ag3):
        phase[4]()
    for kind in range(3):
        x_all(kind).wait_send()


def closing_kernel(ps, srout, l0, xx, right, states, ps_o, sr_o, bs_o, ls_o, sol, sem, sol_sem):
    copies = [
        pltpu.make_async_copy(src, dst, sem.at[i])
        for i, (src, dst) in enumerate([(ps, ps_o), (states, ls_o), (srout, sr_o)])
    ]
    for copy in copies:
        copy.start()
    for b in range(2):
        for m in range(4):
            low, top = m * BLK, (m + 1) * BLK
            sol[b, low:top, :] = (l0[b, low:top, :] + nn(xx[b, low:top, :], right[b])).astype(BF16)
            copy = pltpu.make_async_copy(
                sol.at[b, pl.ds(low, BLK)], bs_o.at[b, pl.ds(low, BLK)], sol_sem.at[4 * b + m]
            )
            copy.start()
            copies.append(copy)
    for copy in copies:
        copy.wait()


def flipped(array):
    return jnp.swapaxes(array, -1, -2)


def shards(
    tile_left, tile_right, row_left, row_right, sketch, panel_left, panel_right,
    pivot_inverse, band_inverse, link_left, link_right, pivot_rhs, band_rhs, carry_in,
):
    args = (
        flipped(tile_left).reshape(128, 1024),
        flipped(tile_right).reshape(128, 1024),
        flipped(row_left).reshape(64, 1024),
        flipped(row_right).reshape(64, 1024),
        flipped(sketch),
        flipped(panel_left).reshape(128, 1024),
        flipped(panel_right).reshape(128, 1024),
        pivot_inverse,
        band_inverse,
        flipped(link_left).reshape(128, 1024),
        flipped(link_right).reshape(128, 1024),
        pivot_rhs,
        band_rhs,
        carry_in,
    )
    vm = pltpu.VMEM
    comm = (64, 16, 128)

    def comm_scratch():
        return [
            vm(comm, F32), vm((32, 16, 128), F32), vm((32, 16, 128), F32),
            vm((8, 3, 16, 128), F32), vm((8, 16, 128), F32), vm((7, 16, 128), F32), vm(comm, F32),
        ]

    scratch = [
        vm((128, 1024), BF16), vm((128, 1024), BF16), vm((64, 1024), BF16), vm((64, 1024), BF16),
        vm((64, 1024), BF16), vm((128, 1024), BF16), vm((128, 1024), BF16), vm((1024, 1024), BF16),
        vm((2, 1024, 1024), BF16), vm((128, 1024), BF16), vm((128, 1024), BF16),
        vm((1024, 512), BF16), vm((2, 1024, 512), BF16), vm((64, 512), F32),
        vm((2, 1024, 512), BF16), vm((1024, 512), BF16), vm((1024, 512), BF16),
        vm((1024, 128), BF16), vm((128, 64), F32),
        vm((2, 128, 1024), BF16), vm((2, 128, 512), BF16),
        vm((2, 64, 64), F32), vm((2, 64, 512), F32),
        *comm_scratch(),
        *comm_scratch(), vm((64, 8, 128), F32),
        vm((2, 64, 1024), F32), vm((2, 128, 1024), BF16), vm((128, 1024), BF16),
        vm((128, 128), F32), vm((256, 128), F32), vm((64, 128), F32), vm((64, 128), F32),
        vm((64, 512), F32), vm((64, 64), F32), vm((3, 64, 512), F32), vm((3, 64, 64), F32),
        vm((16, 128), F32), vm((3, 16, 128), F32), vm((2, 128, 64), F32), vm((64, 512), F32),
    ]
    dma = pltpu.SemaphoreType.DMA
    sems = [
        dma((14,)), dma((2, 8)), dma((2, 8)), dma((2,)), dma((2,)),
        dma((3, 7)), dma((3, 8)), dma((3,)), dma((3,)), dma((3,)), dma((3,)),
    ]
    anywhere = pl.BlockSpec(memory_space=pl.ANY)
    inside = pl.BlockSpec(memory_space=pltpu.VMEM)
    held = pl.pallas_call(
        kernel,
        out_shape=(
            vm((1024, 512), BF16),
            vm((2, 16, 64), F32),
            vm((2, 1024, 512), F32),
            vm((2, 1024, 256), BF16),
            vm((2, 256, 512), BF16),
            vm((2, 64, 512), F32),
        ),
        in_specs=[anywhere] * 14,
        out_specs=(inside,) * 6,
        scratch_shapes=scratch + sems,
        compiler_params=pltpu.CompilerParams(
            collective_id=0, has_side_effects=True, vmem_limit_bytes=KERNEL_VMEM
        ),
        name="panel_update",
    )(*args)
    return pl.pallas_call(
        closing_kernel,
        out_shape=(
            jax.ShapeDtypeStruct((1024, 512), BF16),
            jax.ShapeDtypeStruct((2, 16, 64), F32),
            jax.ShapeDtypeStruct((2, 1024, 512), BF16),
            jax.ShapeDtypeStruct((2, 64, 512), F32),
        ),
        in_specs=[inside] * 6,
        out_specs=(anywhere,) * 4,
        scratch_shapes=[vm((2, 1024, 512), BF16), dma((3,)), dma((8,))],
        compiler_params=pltpu.CompilerParams(vmem_limit_bytes=CLOSING_VMEM),
        name="solutions",
    )(*held)


def solution(mesh):
    return jax.shard_map(
        shards,
        mesh=mesh,
        in_specs=(
            P("col", "row", None, None),
            P("col", "row", None, None),
            P("col", None, None),
            P("col", None, None),
            P(),
            P("row", None, None),
            P("row", None, None),
            P(),
            P("row", None, None),
            P("row", None, None),
            P("row", None, None),
            P(None, "col"),
            P("row", None, "col"),
            P(None, "col"),
        ),
        out_specs=(
            P(None, "col"),
            P("row", "col", None),
            P("row", None, "col"),
            P("row", None, "col"),
        ),
        check_vma=False,
    )
```
